32 devices in a mesh: tensor: 4 (over y, x), context: 2 (over core), dp: 4 (over z).
Axes of the slice: x: 2, y: 2, z: 4, core: 2. Of those that a mesh axis runs over, the one named last changes fastest.
Arguments:
- inputs: bfloat16 [4, 512, 1024], P('dp', 'context'), may hold values from -6 to 6
- norm_gain1: float32 [1024], replicated, may hold values from 0.5 to 1.5
- w_query: bfloat16 [1024, 512], P(None, 'tensor'), may hold values from -0.1875 to 0.1875
- w_key: bfloat16 [1024, 512], P(None, 'tensor'), may hold values from -0.1875 to 0.1875
- w_value: bfloat16 [1024, 1024], P(None, 'tensor'), may hold values from -0.1875 to 0.1875
- w_gate_out: bfloat16 [1024, 1024], P(None, 'tensor'), may hold values from -0.1875 to 0.1875
- w_low_down: bfloat16 [1024, 16], replicated, may hold values from -0.1875 to 0.1875
- w_low_up: bfloat16 [16, 512], P(None, 'tensor'), may hold values from -3 to 3
- forget_bias: float32 [512], P('tensor'), may hold values from -1 to 9, as said below
- head_gain: float32 [256], replicated, may hold values from 0.5 to 1.5
- w_output: bfloat16 [1024, 1024], P('tensor'), may hold values from -0.1875 to 0.1875
- norm_gain2: float32 [1024], replicated, may hold values from 0.5 to 1.5
- w_ffn_gate: bfloat16 [1024, 2816], P(None, 'tensor'), may hold values from -0.1875 to 0.1875
- w_ffn_up: bfloat16 [1024, 2816], P(None, 'tensor'), may hold values from -0.1875 to 0.1875
- w_ffn_down: bfloat16 [2816, 1024], P('tensor'), may hold values from -0.109375 to 0.109375
- cotangent: bfloat16 [4, 512, 1024], P('dp', 'context'), may hold values from -6 to 6
Outputs:
- result: bfloat16 [4, 512, 1024], P('dp', 'context')
- grad_inputs: float32 [4, 512, 1024], P('dp', 'context')
- grad_gain1: float32 [1024], P(('context', 'dp'))
- grad_w_query: float32 [1024, 512], P(('context', 'dp'), 'tensor')
- grad_w_key: float32 [1024, 512], P(('context', 'dp'), 'tensor')
- grad_w_value: float32 [1024, 1024], P(('context', 'dp'), 'tensor')
- grad_w_gate_out: float32 [1024, 1024], P(('context', 'dp'), 'tensor')
- grad_w_low_down: float32 [1024, 16], P(('context', 'dp'))
- grad_w_low_up: float32 [16, 512], P(None, ('tensor', 'context', 'dp'))
- grad_forget_bias: float32 [512], P(('tensor', 'context', 'dp'))
- grad_head_gain: float32 [256], P(('context', 'dp'))
- grad_w_output: float32 [1024, 1024], P('tensor', ('context', 'dp'))
- grad_gain2: float32 [1024], P(('context', 'dp'))
- grad_w_ffn_gate: float32 [1024, 2816], P(('context', 'dp'), 'tensor')
- grad_w_ffn_up: float32 [1024, 2816], P(('context', 'dp'), 'tensor')
- grad_w_ffn_down: float32 [2816, 1024], P('tensor', ('context', 'dp'))
The draws below stay inside these ranges and needn't reach their ends.
Inputs may be any that keep to these rules, and one draw needn't show every extreme that they name: `forget_bias`: bias of the forget gate's logits, one per key channel.
All inputs are finite; a program needn't handle non-finite values.
Results may differ from the reference program's by a relative error of at most 0.012.
The reference program's roundings to bfloat16 on the way (of `normed_one`, `gated`, `normed_two`, `mixed_act` and `grad_attn`) count: a program that leaves them out, or rounds other values in their place, can miss the bound.
Values sent between devices are 32-bit elements; how exact they have to be, the bound alone decides.
A program may use at most 128 MiB of HBM per device.

```python
import jax
import jax.numpy as jnp
from jax import lax

D = 1024
HEADS = 4
KEY = 128
VAL = 256
FF = 2816
RANK = 16
BLOCK = 64
SEQS = 4
LEN = 512
KEY_ALL = 512
VAL_ALL = 1024


def draw_forget_bias(key, part):
    return jax.random.uniform(key, (KEY_ALL,), jnp.float32, -1.0, 8.0)


def block_levels(own_key, dims, pieces, least, top_value):
    loudness = 1.0
    for dim, parts in pieces:
        heights = jax.random.uniform(jax.random.fold_in(jax.random.fold_in(own_key, 6), dim), (parts,), jnp.float32, least / len(pieces), top_value / len(pieces))
        loudness = loudness * jnp.repeat(jnp.exp(heights), dims[dim] // parts).reshape((-1,) + (1,) * (len(dims) - 1 - dim))
    return loudness


def normal_values(rng, extent, scale, limit, cuts=(), kind=jnp.bfloat16):
    array = scale * jax.random.normal(rng, extent, jnp.float32)
    if cuts:
        array = array * block_levels(rng, extent, cuts, -0.22, 0.18)
    return jnp.clip(array, -limit, limit).astype(kind)


def setup_inputs(seed: int = 0) -> dict:
    key_of = jax.random.split(jax.random.key(seed), 17)
    return {
        "inputs": normal_values(key_of[0], (SEQS, LEN, D), 1.0, 6.0, ((0, 4), (1, 2))),
        "norm_gain1": jnp.clip(1.0 + 0.1 * jax.random.normal(key_of[1], (D,), jnp.float32), 0.5, 1.5),
        "w_query": normal_values(key_of[2], (D, KEY_ALL), D ** -0.5, 0.1875, ((1, 4),)),
        "w_key": normal_values(key_of[3], (D, KEY_ALL), D ** -0.5, 0.1875, ((1, 4),)),
        "w_value": normal_values(key_of[4], (D, VAL_ALL), D ** -0.5, 0.1875, ((1, 4),)),
        "w_gate_out": normal_values(key_of[5], (D, VAL_ALL), D ** -0.5, 0.1875, ((1, 4),)),
        "w_low_down": normal_values(key_of[6], (D, RANK), D ** -0.5, 0.1875),
        "w_low_up": normal_values(key_of[7], (RANK, KEY_ALL), (RANK // 4) ** -0.5, 3.0, ((1, 4),)),
        "forget_bias": draw_forget_bias(jax.random.fold_in(key_of[16], 71), 0),
        "head_gain": jnp.clip(1.0 + 0.1 * jax.random.normal(key_of[9], (VAL,), jnp.float32), 0.5, 1.5),
        "w_output": normal_values(key_of[10], (VAL_ALL, D), VAL_ALL ** -0.5, 0.1875, ((0, 4),)),
        "norm_gain2": jnp.clip(1.0 + 0.1 * jax.random.normal(key_of[11], (D,), jnp.float32), 0.5, 1.5),
        "w_ffn_gate": normal_values(key_of[12], (D, FF), D ** -0.5, 0.1875, ((1, 4),)),
        "w_ffn_up": normal_values(key_of[13], (D, FF), D ** -0.5, 0.1875, ((1, 4),)),
        "w_ffn_down": normal_values(key_of[14], (FF, D), FF ** -0.5, 0.109375, ((0, 4),)),
        "cotangent": normal_values(key_of[15], (SEQS, LEN, D), 1.0, 6.0, ((0, 4), (1, 2))),
    }


EPS_MODEL = 1e-06
EPS_HEAD = 1e-05
GATE_NORM = 16.0
HIGHEST = lax.Precision.HIGHEST

def block_step(carried, block_in):
    queries, keys_in, values_in, log_rates = block_in
    cumul_log = jnp.cumsum(log_rates, axis=0)
    anchor = 0.5 * cumul_log[-1]
    scores = jnp.dot(queries * jnp.exp(cumul_log - anchor), (keys_in * jnp.exp(anchor - cumul_log)).T, precision=HIGHEST)
    length = queries.shape[0]
    causal = jnp.arange(length)[:, None] >= jnp.arange(length)[None, :]
    scores = jnp.where(causal, scores, 0.0)
    outputs = jnp.dot(scores, values_in, precision=HIGHEST) + jnp.dot(queries * jnp.exp(cumul_log), carried, precision=HIGHEST)
    end_log = cumul_log[-1]
    updated = jnp.exp(end_log)[:, None] * carried + jnp.dot((keys_in * jnp.exp(end_log - cumul_log)).T, values_in, precision=HIGHEST)
    return (updated, outputs)

def gla_core(queries, keys_in, values_in, log_rates, initial):
    block_count = queries.shape[0] // BLOCK
    blocks = (queries.reshape(block_count, BLOCK, -1), keys_in.reshape(block_count, BLOCK, -1), values_in.reshape(block_count, BLOCK, -1), log_rates.reshape(block_count, BLOCK, -1))
    final_state, outputs = lax.scan(block_step, initial, blocks)
    return (outputs.reshape(queries.shape[0], -1), final_state)

def rms_scale(rows_in):
    return lax.rsqrt(lax.optimization_barrier(jnp.mean(rows_in * rows_in, axis=-1, keepdims=True)) + EPS_MODEL)

def norm_back(rows_in, scale_rows, gain_in, grad_normed):
    weighted = gain_in * grad_normed
    grad_gain = lax.optimization_barrier(jnp.sum(grad_normed * rows_in * scale_rows, axis=0))
    grad_rows = scale_rows * (weighted - rows_in * scale_rows * scale_rows * lax.optimization_barrier(jnp.mean(weighted * rows_in, axis=-1, keepdims=True)))
    return (grad_rows, grad_gain)

def head_gate(outputs, head_gain, gate_in):
    scale_rows = lax.rsqrt(lax.optimization_barrier(jnp.mean(outputs * outputs, axis=-1, keepdims=True)) + EPS_HEAD)
    return outputs * scale_rows * head_gain * jax.nn.silu(gate_in)

def silu_grad(values_in):
    sigmoid_v = jax.nn.sigmoid(values_in)
    return sigmoid_v * (1.0 + values_in * (1.0 - sigmoid_v))

def reference(inputs, norm_gain1, w_query, w_key, w_value, w_gate_out, w_low_down, w_low_up, forget_bias, head_gain, w_output, norm_gain2, w_ffn_gate, w_ffn_up, w_ffn_down, cotangent):
    key_scale = KEY ** (-0.5)
    core_heads = jax.vmap(gla_core)
    bf16 = jnp.bfloat16
    f32 = jnp.float32

    def to_heads(packed, width_head):
        return packed.reshape(LEN, HEADS, width_head).transpose(1, 0, 2)

    def from_heads(packed):
        return packed.transpose(1, 0, 2).reshape(LEN, -1)

    def one_sequence(totals, seq_pair):
        seq_in, seq_cot = seq_pair
        rows_in = seq_in.astype(f32)
        scale_one = rms_scale(rows_in)
        normed_one = (rows_in * scale_one * norm_gain1).astype(bf16)
        queries = jnp.dot(normed_one, w_query, preferred_element_type=f32) * key_scale
        keys_proj = jnp.dot(normed_one, w_key, preferred_element_type=f32)
        values_proj = jnp.dot(normed_one, w_value, preferred_element_type=f32)
        gate_in = jnp.dot(normed_one, w_gate_out, preferred_element_type=f32)
        low_rank = jnp.dot(normed_one, w_low_down, preferred_element_type=f32)
        logits = jnp.dot(low_rank, w_low_up.astype(f32), precision=HIGHEST) + forget_bias
        log_rates = jax.nn.log_sigmoid(logits) / GATE_NORM
        initial = jnp.zeros((HEADS, KEY, VAL), f32)
        core_out, core_pull = jax.vjp(core_heads, to_heads(queries, KEY), to_heads(keys_proj, KEY), to_heads(values_proj, VAL), to_heads(log_rates, KEY), initial)
        outputs = core_out[0].transpose(1, 0, 2)
        gate_heads = gate_in.reshape(LEN, HEADS, VAL)
        gated, gate_pull = jax.vjp(head_gate, outputs, head_gain, gate_heads)
        gated_bf = gated.reshape(LEN, VAL_ALL).astype(bf16)
        hidden_res = rows_in + jnp.dot(gated_bf, w_output, preferred_element_type=f32)
        scale_two = rms_scale(hidden_res)
        normed_two = (hidden_res * scale_two * norm_gain2).astype(bf16)
        ffn_gate = jnp.dot(normed_two, w_ffn_gate, preferred_element_type=f32)
        ffn_up = jnp.dot(normed_two, w_ffn_up, preferred_element_type=f32)
        mixed_act = (jax.nn.silu(ffn_gate) * ffn_up).astype(bf16)
        result = hidden_res + jnp.dot(mixed_act, w_ffn_down, preferred_element_type=f32)
        grad_res = seq_cot.astype(f32)
        grad_down = jnp.dot(mixed_act.T, seq_cot, preferred_element_type=f32)
        grad_mixed = jnp.dot(seq_cot, w_ffn_down.T, preferred_element_type=f32)
        grad_gate = (grad_mixed * ffn_up * silu_grad(ffn_gate)).astype(bf16)
        grad_up = (grad_mixed * jax.nn.silu(ffn_gate)).astype(bf16)
        grad_ffn_gate = jnp.dot(normed_two.T, grad_gate, preferred_element_type=f32)
        grad_ffn_up = jnp.dot(normed_two.T, grad_up, preferred_element_type=f32)
        grad_normed_two = jnp.dot(grad_gate, w_ffn_gate.T, preferred_element_type=f32) + jnp.dot(grad_up, w_ffn_up.T, preferred_element_type=f32)
        grad_two_rows, grad_gain_two = norm_back(hidden_res, scale_two, norm_gain2, grad_normed_two)
        grad_hidden = grad_res + grad_two_rows
        grad_attn = grad_hidden.astype(bf16)
        grad_out_proj = jnp.dot(gated_bf.T, grad_attn, preferred_element_type=f32)
        grad_gated = jnp.dot(grad_attn, w_output.T, preferred_element_type=f32).reshape(LEN, HEADS, VAL)
        grad_outputs, grad_gain_head, grad_gate_heads = gate_pull(grad_gated)
        grad_q_h, grad_k_h, grad_v_h, grad_lr_h, unused_state = core_pull((grad_outputs.transpose(1, 0, 2), jnp.zeros_like(core_out[1])))
        grad_logits = from_heads(grad_lr_h) * jax.nn.sigmoid(-logits) / GATE_NORM
        grad_bias = lax.optimization_barrier(jnp.sum(grad_logits, axis=0))
        grad_low_up = jnp.dot(low_rank.T, grad_logits, precision=HIGHEST)
        grad_low = jnp.dot(grad_logits, w_low_up.astype(f32).T, precision=HIGHEST)
        grad_low_down = jnp.dot(normed_one.astype(f32).T, grad_low, precision=HIGHEST)
        grad_q = (from_heads(grad_q_h) * key_scale).astype(bf16)
        grad_k = from_heads(grad_k_h).astype(bf16)
        grad_v = from_heads(grad_v_h).astype(bf16)
        grad_g = grad_gate_heads.reshape(LEN, VAL_ALL).astype(bf16)
        grad_query_w = jnp.dot(normed_one.T, grad_q, preferred_element_type=f32)
        grad_key_w = jnp.dot(normed_one.T, grad_k, preferred_element_type=f32)
        grad_value_w = jnp.dot(normed_one.T, grad_v, preferred_element_type=f32)
        grad_gate_w = jnp.dot(normed_one.T, grad_g, preferred_element_type=f32)
        grad_normed_one = jnp.dot(grad_q, w_query.T, preferred_element_type=f32) + jnp.dot(grad_k, w_key.T, preferred_element_type=f32) + jnp.dot(grad_v, w_value.T, preferred_element_type=f32) + jnp.dot(grad_g, w_gate_out.T, preferred_element_type=f32) + jnp.dot(grad_low, w_low_down.astype(f32).T, precision=HIGHEST)
        grad_one_rows, grad_gain_one = norm_back(rows_in, scale_one, norm_gain1, grad_normed_one)
        grad_in = grad_hidden + grad_one_rows
        new_terms = (grad_gain_one, grad_query_w, grad_key_w, grad_value_w, grad_gate_w, grad_low_down, grad_low_up, grad_bias, grad_gain_head, grad_out_proj, grad_gain_two, grad_ffn_gate, grad_ffn_up, grad_down)
        new_totals = tuple((old + new for old, new in zip(totals, new_terms)))
        return (new_totals, (result.astype(bf16), grad_in))
    start_totals = tuple((jnp.zeros(shaped.shape, f32) for shaped in (norm_gain1, w_query, w_key, w_value, w_gate_out, w_low_down, w_low_up, forget_bias, head_gain, w_output, norm_gain2, w_ffn_gate, w_ffn_up, w_ffn_down)))
    totals, (results, grads_in) = lax.scan(one_sequence, start_totals, (inputs, cotangent))
    grad_gain1, grad_w_query, grad_w_key, grad_w_value, grad_w_gate_out, grad_w_low_down, grad_w_low_up, grad_forget_bias, grad_head_gain, grad_w_output, grad_gain2, grad_w_ffn_gate, grad_w_ffn_up, grad_w_ffn_down = totals
    return (results, grads_in, grad_gain1, grad_w_query, grad_w_key, grad_w_value, grad_w_gate_out, grad_w_low_down, grad_w_low_up, grad_forget_bias, grad_head_gain, grad_w_output, grad_gain2, grad_w_ffn_gate, grad_w_ffn_up, grad_w_ffn_down)
```

```python
import functools

import jax
import jax.numpy as jnp
from jax import lax
from jax.experimental import pallas as pl
from jax.experimental.pallas import tpu as pltpu
from jax.sharding import PartitionSpec as P

BLOCK = 64


EPS_MODEL = 1e-06
EPS_HEAD = 1e-05
GATE_NORM = 16.0
HIGHEST = lax.Precision.HIGHEST


VMEM_LIMIT = 60 * 1024 * 1024
VMEM = pltpu.MemorySpace.VMEM
MESH_ID = pl.DeviceIdType.MESH


def hdot(left, right, dims):
    return lax.dot_general(
        left, right, (dims, ((), ())), precision=HIGHEST, preferred_element_type=jnp.float32
    )


def column_of(row, height):
    return jnp.broadcast_to(row, (height, row.shape[1])).T


def triangle(length):
    rows = lax.broadcasted_iota(jnp.int32, (length, length), 0)
    cols = lax.broadcasted_iota(jnp.int32, (length, length), 1)
    return rows >= cols


def gla_forward_kernel(q_ref, k_ref, v_ref, r_ref, out_ref, decayed_ref, states_ref, pair_ref):
    tokens, key_dim = q_ref.shape
    value_dim = v_ref.shape[1]
    causal = triangle(BLOCK)
    ones_low = causal.astype(jnp.float32)
    state = jnp.zeros((key_dim, value_dim), jnp.float32)
    before = jnp.zeros((1, key_dim), jnp.float32)
    for block in range(tokens // BLOCK):
        span = pl.ds(block * BLOCK, BLOCK)
        queries, keys_in, values_in = q_ref[span, :], k_ref[span, :], v_ref[span, :]
        cumul = hdot(ones_low, r_ref[span, :], ((1,), (0,)))
        end_log = cumul[BLOCK - 1 :, :]
        anchor = 0.5 * end_log
        scores = hdot(
            queries * jnp.exp(cumul - anchor), keys_in * jnp.exp(anchor - cumul), ((1,), (1,))
        )
        scores = jnp.where(causal, scores, 0.0)
        out_ref[span, :] = hdot(scores, values_in, ((1,), (0,))) + hdot(
            queries * jnp.exp(cumul), state, ((1,), (0,))
        )
        decayed_ref[span, :] = queries * jnp.exp(cumul + before)
        states_ref[block] = state
        added = hdot(keys_in * jnp.exp(end_log - cumul), values_in, ((0,), (0,)))
        state = column_of(jnp.exp(end_log), key_dim)[:, :1] * state + added
        before = before + end_log
    pair_ref[:, :value_dim] = state
    pair_ref[:, value_dim:] = column_of(jnp.exp(before), key_dim)


def gla_forward(queries, keys_in, values_in, log_rates):
    tokens, key_dim = queries.shape
    value_dim = values_in.shape[1]
    f32 = jnp.float32
    return pl.pallas_call(
        gla_forward_kernel,
        out_shape=(
            jax.ShapeDtypeStruct((tokens, value_dim), f32),
            jax.ShapeDtypeStruct((tokens, key_dim), f32),
            jax.ShapeDtypeStruct((tokens // BLOCK, key_dim, value_dim), f32),
            jax.ShapeDtypeStruct((key_dim, value_dim + key_dim), f32),
        ),
        compiler_params=pltpu.CompilerParams(vmem_limit_bytes=VMEM_LIMIT),
        name="gla_forward",
    )(queries, keys_in, values_in, log_rates)


def gla_backward_kernel(
    q_ref, k_ref, v_ref, r_ref, states_ref, entry_ref, later_ref, g_ref, dq_ref, dk_ref, dv_ref, dr_ref
):
    tokens, key_dim = q_ref.shape
    causal = triangle(BLOCK)
    ones_low = causal.astype(jnp.float32)
    blocks = tokens // BLOCK
    cumuls, befores = [], []
    before = jnp.zeros((1, key_dim), jnp.float32)
    for block in range(blocks):
        cumul = hdot(ones_low, r_ref[pl.ds(block * BLOCK, BLOCK), :], ((1,), (0,)))
        cumuls.append(cumul)
        befores.append(before)
        before = before + cumul[BLOCK - 1 :, :]
    grad_state = later_ref[...]
    entry = entry_ref[...]
    for block in reversed(range(blocks)):
        span = pl.ds(block * BLOCK, BLOCK)
        queries, keys_in, values_in = q_ref[span, :], k_ref[span, :], v_ref[span, :]
        grad_out = g_ref[span, :]
        cumul = cumuls[block]
        end_log = cumul[BLOCK - 1 :, :]
        anchor = 0.5 * end_log
        state = states_ref[block] + column_of(jnp.exp(befores[block]), key_dim)[:, :1] * entry
        up, down = jnp.exp(cumul - anchor), jnp.exp(anchor - cumul)
        grow, rest = jnp.exp(cumul), jnp.exp(end_log - cumul)
        q_up, k_down = queries * up, keys_in * down
        scores = jnp.where(causal, hdot(q_up, k_down, ((1,), (1,))), 0.0)
        grad_scores = jnp.where(causal, hdot(grad_out, values_in, ((1,), (1,))), 0.0)
        grad_q = hdot(grad_scores, k_down, ((1,), (0,))) * up + grow * hdot(
            grad_out, state, ((1,), (1,))
        )
        carried_k = hdot(values_in, grad_state, ((1,), (1,))) * rest
        grad_k = hdot(grad_scores, q_up, ((0,), (0,))) * down + carried_k
        dv_ref[span, :] = hdot(scores, grad_out, ((0,), (0,))) + hdot(
            keys_in * rest, grad_state, ((1,), (0,))
        )
        dq_ref[span, :] = grad_q
        dk_ref[span, :] = grad_k
        grad_cumul = queries * grad_q - keys_in * grad_k
        end_column = column_of(jnp.exp(end_log), key_dim)
        state_term = jnp.sum(grad_state * state, axis=1, keepdims=True) * end_column
        grad_end = state_term.T[:1, :] + jnp.sum(carried_k * keys_in, axis=0, keepdims=True)
        dr_ref[span, :] = hdot(ones_low, grad_cumul, ((0,), (0,))) + grad_end
        grad_state = end_column[:, :1] * grad_state + hdot(
            queries * grow, grad_out, ((0,), (0,))
        )


def gla_backward(queries, keys_in, values_in, log_rates, states, entry, later, grad_out):
    shaped = tuple(
        jax.ShapeDtypeStruct(part.shape, jnp.float32)
        for part in (queries, keys_in, values_in, log_rates)
    )
    return pl.pallas_call(
        gla_backward_kernel,
        out_shape=shaped,
        compiler_params=pltpu.CompilerParams(vmem_limit_bytes=VMEM_LIMIT),
        name="gla_backward",
    )(queries, keys_in, values_in, log_rates, states, entry, later, grad_out)


def exchange_kernel(size, reverse, value_dim, pair_ref, out_ref, slots, send_sem, recv_sem):
    here = lax.axis_index("context")
    barrier = pltpu.get_barrier_semaphore()
    for step in range(1, size):
        peer = lax.rem(here + step, size)
        pl.semaphore_signal(barrier, inc=1, device_id={"context": peer}, device_id_type=MESH_ID)
    pl.semaphore_wait(barrier, size - 1)
    copies = []
    for step in range(1, size):
        peer = lax.rem(here + step, size)
        copies.append(
            pltpu.make_async_remote_copy(
                src_ref=pair_ref,
                dst_ref=slots.at[step - 1],
                send_sem=send_sem.at[step - 1],
                recv_sem=recv_sem.at[step - 1],
                device_id={"context": peer},
                device_id_type=MESH_ID,
            )
        )
    for copy in copies:
        copy.start()
    for copy in copies:
        copy.wait()
    out_ref[...] = jnp.zeros_like(out_ref)
    order = range(1, size) if reverse else reversed(range(1, size))
    if reverse:
        for m in reversed(range(1, size)):

            @pl.when(here + m < size)
            def _(m=m):
                part = slots.at[size - m - 1]
                out_ref[...] = part[:, value_dim : value_dim + 1] * out_ref[...] + part[:, :value_dim]
    else:
        for step in order:

            @pl.when(here >= step)
            def _(step=step):
                part = slots.at[step - 1]
                out_ref[...] = part[:, value_dim : value_dim + 1] * out_ref[...] + part[:, :value_dim]


def exchange(pair, value_dim, reverse, collective_id):
    size = lax.axis_size("context")
    return pl.pallas_call(
        functools.partial(exchange_kernel, size, reverse, value_dim),
        out_shape=jax.ShapeDtypeStruct((pair.shape[0], value_dim), jnp.float32),
        in_specs=[pl.BlockSpec(memory_space=VMEM)],
        out_specs=pl.BlockSpec(memory_space=VMEM),
        scratch_shapes=[
            pltpu.VMEM((size - 1,) + pair.shape, jnp.float32),
            pltpu.SemaphoreType.DMA((size - 1,)),
            pltpu.SemaphoreType.DMA((size - 1,)),
        ],
        compiler_params=pltpu.CompilerParams(
            collective_id=collective_id, has_side_effects=True, vmem_limit_bytes=VMEM_LIMIT
        ),
        name="exchange_back" if reverse else "exchange",
    )(pair)


def sums_kernel(sizes, n_all, pieces, tail, *refs):
    n_ctx, n_dp, n_ten = sizes
    n_sc = len(pieces)
    take = iter(refs)
    all_in = [next(take) for _ in range(n_all)]
    sc_in = [next(take) for _ in range(n_sc)]
    all_out = [next(take) for _ in range(n_all)]
    sc_out = [next(take) for _ in range(n_sc)]
    all_slots = [next(take) for _ in range(n_all)]
    all_sems = [next(take) for _ in range(n_all)]
    near = [next(take) for _ in range(n_sc)]
    near_sems = [next(take) for _ in range(n_sc)]
    line = [next(take) for _ in range(n_sc)]
    line_sems = [next(take) for _ in range(n_sc)]
    if tail:
        tail_slots, tail_sems = next(take), next(take)
    ctx = lax.axis_index("context")
    dp = lax.axis_index("dp")
    ten = lax.axis_index("tensor")
    use_ten = n_all > 0 or tail

    def peers(index, size):
        return [lax.rem(index + step, size) for step in range(1, size)]

    def remote(src, dst, sems, at, axis, peer):
        return pltpu.make_async_remote_copy(
            src_ref=src,
            dst_ref=dst,
            send_sem=sems.at[(0,) + at],
            recv_sem=sems.at[(1,) + at],
            device_id={axis: peer},
            device_id_type=MESH_ID,
        )

    barrier = pltpu.get_barrier_semaphore()

    def greet(axis, peer):
        pl.semaphore_signal(barrier, inc=1, device_id={axis: peer}, device_id_type=MESH_ID)

    expect = 0
    if n_sc:
        for peer in peers(ctx, n_ctx):
            greet("context", peer)
        expect += n_ctx - 1
    if use_ten:
        for peer in peers(ten, n_ten):
            greet("tensor", peer)
        expect += n_ten - 1
    if n_sc:

        @pl.when(dp > 0)
        def _():
            greet("dp", dp - 1)

        @pl.when(dp < n_dp - 1)
        def _():
            greet("dp", dp + 1)

    if n_sc:
        inner = jnp.logical_and(dp > 0, dp < n_dp - 1)

        @pl.when(inner)
        def _():
            pl.semaphore_wait(barrier, expect + 2)

        @pl.when(jnp.logical_not(inner))
        def _():
            pl.semaphore_wait(barrier, expect + 1)

    else:
        pl.semaphore_wait(barrier, expect)

    def rows(i, piece):
        height = sc_in[i].shape[1] // pieces[i]
        return pl.ds(piece * height, height)

    def near_copy(i, step, dest, piece):
        peer = lax.rem(ctx + step, n_ctx)
        return remote(
            sc_in[i].at[peer * n_dp + dest, rows(i, piece)],
            near[i].at[step - 1, dest, rows(i, piece)],
            near_sems[i],
            (step - 1, dest, piece),
            "context",
            peer,
        )

    def line_copy(i, way, dest, piece, peer):
        place = line[i].at[way, dest, rows(i, piece)]
        return remote(place, place, line_sems[i], (way, dest, piece), "dp", peer)

    def all_copy(i, step):
        peer = lax.rem(ten + step, n_ten)
        return remote(
            all_in[i].at[peer], all_slots[i].at[step - 1], all_sems[i], (0, step - 1), "tensor", peer
        )

    def all_share(i, step):
        peer = lax.rem(ten + step, n_ten)
        return remote(
            all_out[i].at[ten], all_out[i].at[ten], all_sems[i], (1, step - 1), "tensor", peer
        )

    def over_pieces(i, body):
        if pieces[i] == 1:
            body(0)
        else:

            def lap(piece, carry):
                body(piece)
                return carry

            lax.fori_loop(0, pieces[i], lap, 0)

    order = []
    for k in range(n_dp):
        for dest in (n_dp - 1 - k, k):
            if dest not in order:
                order.append(dest)
    for i in range(n_all):
        for step in range(1, n_ten):
            all_copy(i, step).start()
    for dest in order:
        for i in range(n_sc):
            for step in range(1, n_ctx):
                over_pieces(i, lambda piece: near_copy(i, step, dest, piece).start())

    def own_sum(i, dest, piece):
        total = sc_in[i][ctx * n_dp + dest, rows(i, piece)]
        for step in range(1, n_ctx):
            near_copy(i, step, dest, piece).wait_recv()
            total = total + near[i][step - 1, dest, rows(i, piece)]
        return total

    def pass_on(i, way, dest, piece):
        forward = way == 0
        active = dp < dest if forward else dp > dest
        first = dp == (0 if forward else n_dp - 1)
        peer = dp + 1 if forward else dp - 1
        back = dp - 1 if forward else dp + 1

        @pl.when(active)
        def _():
            own = own_sum(i, dest, piece)

            @pl.when(first)
            def _():
                line[i][way, dest, rows(i, piece)] = own

            @pl.when(jnp.logical_not(first))
            def _():
                line_copy(i, way, dest, piece, back).wait_recv()
                line[i][way, dest, rows(i, piece)] = line[i][way, dest, rows(i, piece)] + own

            line_copy(i, way, dest, piece, peer).start()

    def reduce_all():
        for i in range(n_all):
            total = all_in[i][ten]
            for step in range(1, n_ten):
                all_copy(i, step).wait_recv()
                total = total + all_slots[i][step - 1]
            all_out[i][ten] = total
            for step in range(1, n_ten):
                all_share(i, step).start()

    if not n_sc:
        reduce_all()
    else:
        for k in range(n_dp - 1):

            def both(piece, i, k=k):
                pass_on(i, 0, n_dp - 1 - k, piece)
                pass_on(i, 1, k, piece)

            for i in range(n_sc):
                over_pieces(i, functools.partial(both, i=i))
            if k == 0:
                reduce_all()

    for i in range(n_sc):

        def finish(piece, i=i):
            sc_out[i][rows(i, piece), :] = own_sum(i, dp, piece)

            @pl.when(dp > 0)
            def _():
                line_copy(i, 0, dp, piece, dp - 1).wait_recv()
                sc_out[i][rows(i, piece), :] += line[i][0, dp, rows(i, piece)]

            @pl.when(dp < n_dp - 1)
            def _():
                line_copy(i, 1, dp, piece, dp + 1).wait_recv()
                sc_out[i][rows(i, piece), :] += line[i][1, dp, rows(i, piece)]

        over_pieces(i, finish)

    if tail:
        last = sc_out[n_sc - 1]
        tail_slots[ten] = last[:tail, :]

        def tail_copy(step):
            peer = lax.rem(ten + step, n_ten)
            return remote(
                tail_slots.at[ten], tail_slots.at[ten], tail_sems, (step - 1,), "tensor", peer
            )

        def tail_come(step):
            sender = lax.rem(ten + n_ten - step, n_ten)
            return remote(
                tail_slots.at[sender], tail_slots.at[sender], tail_sems, (step - 1,), "tensor", sender
            )

        for step in range(1, n_ten):
            tail_copy(step).start()
        for step in range(1, n_ten):
            tail_come(step).wait_recv()
        total = tail_slots[0]
        for index in range(1, n_ten):
            total = total + tail_slots[index]
        last[:tail, :] = total
        for step in range(1, n_ten):
            tail_copy(step).wait_send()

    for i in range(n_all):
        for step in range(1, n_ten):
            all_copy(i, step).wait_send()
            sender = lax.rem(ten + n_ten - step, n_ten)
            remote(
                all_out[i].at[sender],
                all_out[i].at[sender],
                all_sems[i],
                (1, step - 1),
                "tensor",
                sender,
            ).wait_recv()
            all_share(i, step).wait_send()
    for i in range(n_sc):
        for dest in range(n_dp):

            def drain(piece, i=i, dest=dest):
                for step in range(1, n_ctx):
                    near_copy(i, step, dest, piece).wait_send()

                @pl.when(dp < dest)
                def _():
                    line_copy(i, 0, dest, piece, dp + 1).wait_send()

                @pl.when(dp > dest)
                def _():
                    line_copy(i, 1, dest, piece, dp - 1).wait_send()

            over_pieces(i, drain)


def summed_arrays(whole, scattered, tail, collective_id, name):
    n_ctx, n_dp, n_ten = (lax.axis_size(axis) for axis in ("context", "dp", "tensor"))
    owners = n_ctx * n_dp
    f32 = jnp.float32
    whole_in = [part.reshape(n_ten, part.shape[0] // n_ten, part.shape[1]) for part in whole]
    sc_in = [part.reshape(owners, part.shape[0] // owners, part.shape[1]) for part in scattered]
    pieces = []
    for part in sc_in:
        count = 4
        while part.shape[1] % (count * 8):
            count //= 2
        pieces.append(count if part.shape[2] > 128 else 1)
    scratch = [pltpu.VMEM((n_ten - 1,) + part.shape[1:], f32) for part in whole_in]
    scratch += [pltpu.SemaphoreType.DMA((2, 2, n_ten - 1)) for _ in whole_in]
    scratch += [pltpu.VMEM((n_ctx - 1, n_dp) + part.shape[1:], f32) for part in sc_in]
    scratch += [pltpu.SemaphoreType.DMA((2, n_ctx - 1, n_dp, count)) for count in pieces]
    scratch += [pltpu.VMEM((2, n_dp) + part.shape[1:], f32) for part in sc_in]
    scratch += [pltpu.SemaphoreType.DMA((2, 2, n_dp, count)) for count in pieces]
    if tail:
        scratch += [
            pltpu.VMEM((n_ten, tail, scattered[-1].shape[1]), f32),
            pltpu.SemaphoreType.DMA((2, n_ten - 1)),
        ]
    outs = pl.pallas_call(
        functools.partial(sums_kernel, (n_ctx, n_dp, n_ten), len(whole), tuple(pieces), tail),
        out_shape=tuple(
            [jax.ShapeDtypeStruct(part.shape, f32) for part in whole_in]
            + [jax.ShapeDtypeStruct(part.shape[1:], f32) for part in sc_in]
        ),
        in_specs=[pl.BlockSpec(memory_space=VMEM)] * (len(whole) + len(scattered)),
        out_specs=tuple([pl.BlockSpec(memory_space=VMEM)] * (len(whole) + len(scattered))),
        scratch_shapes=scratch,
        compiler_params=pltpu.CompilerParams(
            collective_id=collective_id, has_side_effects=True, vmem_limit_bytes=VMEM_LIMIT
        ),
        name=name,
    )(*whole_in, *sc_in)
    totals = [out.reshape(part.shape) for out, part in zip(outs, whole)]
    return totals, list(outs[len(whole) :])


def rms_scale(rows_in):
    return lax.rsqrt(jnp.mean(rows_in * rows_in, axis=-1, keepdims=True) + EPS_MODEL)


def norm_back(rows_in, scale_rows, gain_in, grad_normed):
    weighted = gain_in * grad_normed
    grad_gain = jnp.sum(grad_normed * rows_in * scale_rows, axis=0)
    grad_rows = scale_rows * (
        weighted
        - rows_in * scale_rows * scale_rows * jnp.mean(weighted * rows_in, axis=-1, keepdims=True)
    )
    return (grad_rows, grad_gain)


def head_gate(outputs, head_gain, gate_in):
    scale_rows = lax.rsqrt(jnp.mean(outputs * outputs, axis=-1, keepdims=True) + EPS_HEAD)
    return outputs * scale_rows * head_gain * jax.nn.silu(gate_in)


def silu_grad(values_in):
    sigmoid_v = jax.nn.sigmoid(values_in)
    return sigmoid_v * (1.0 + values_in * (1.0 - sigmoid_v))


def shards(
    inputs,
    norm_gain1,
    w_query,
    w_key,
    w_value,
    w_gate_out,
    w_low_down,
    w_low_up,
    forget_bias,
    head_gain,
    w_output,
    norm_gain2,
    w_ffn_gate,
    w_ffn_up,
    w_ffn_down,
    cotangent,
):
    bf16 = jnp.bfloat16
    f32 = jnp.float32
    seqs_here, tok_here, model_width = inputs.shape
    value_dim = head_gain.shape[0]
    heads_here = w_output.shape[0] // value_dim
    key_dim = w_query.shape[1] // heads_here
    key_scale = key_dim ** (-0.5)
    rows_in = inputs.reshape(-1, model_width).astype(f32)
    scale_one = rms_scale(rows_in)
    normed_one = (rows_in * scale_one * norm_gain1).astype(bf16)
    queries = jnp.dot(normed_one, w_query, preferred_element_type=f32) * key_scale
    keys_proj = jnp.dot(normed_one, w_key, preferred_element_type=f32)
    values_proj = jnp.dot(normed_one, w_value, preferred_element_type=f32)
    gate_in = jnp.dot(normed_one, w_gate_out, preferred_element_type=f32)
    low_rank = jnp.dot(normed_one, w_low_down, preferred_element_type=f32)
    logits = jnp.dot(low_rank, w_low_up.astype(f32), precision=HIGHEST) + forget_bias
    log_rates = jax.nn.log_sigmoid(logits) / GATE_NORM
    pairs = [(s, h) for s in range(seqs_here) for h in range(heads_here)]

    def one(packed, s, h, width):
        return packed[s * tok_here : (s + 1) * tok_here, h * width : (h + 1) * width]

    def join(parts):
        return jnp.concatenate(
            [
                jnp.concatenate(parts[s * heads_here : (s + 1) * heads_here], axis=1)
                for s in range(seqs_here)
            ],
            axis=0,
        )

    def stacked(parts):
        return jnp.concatenate(parts, axis=0)

    cores = [
        gla_forward(
            one(queries, s, h, key_dim),
            one(keys_proj, s, h, key_dim),
            one(values_proj, s, h, value_dim),
            one(log_rates, s, h, key_dim),
        )
        for s, h in pairs
    ]
    pair_all = stacked([core[3] for core in cores])
    entry_all = exchange(pair_all, value_dim, False, 0)
    entries = [entry_all[i * key_dim : (i + 1) * key_dim] for i in range(len(pairs))]
    outputs = join(
        [
            core[0] + jnp.dot(core[1], entry, precision=HIGHEST)
            for core, entry in zip(cores, entries)
        ]
    ).reshape(-1, heads_here, value_dim)
    gate_heads = gate_in.reshape(-1, heads_here, value_dim)
    gated, gate_pull = jax.vjp(head_gate, outputs, head_gain, gate_heads)
    gated_bf = gated.reshape(-1, heads_here * value_dim).astype(bf16)
    attn_part_out = jnp.dot(gated_bf, w_output, preferred_element_type=f32)
    (attn_sum,), _ = summed_arrays([attn_part_out], [], 0, 1, "sum_attn")
    hidden_res = rows_in + attn_sum
    scale_two = rms_scale(hidden_res)
    normed_two = (hidden_res * scale_two * norm_gain2).astype(bf16)
    ffn_gate = jnp.dot(normed_two, w_ffn_gate, preferred_element_type=f32)
    ffn_up = jnp.dot(normed_two, w_ffn_up, preferred_element_type=f32)
    mixed_act = (jax.nn.silu(ffn_gate) * ffn_up).astype(bf16)
    ffn_down_part = jnp.dot(mixed_act, w_ffn_down, preferred_element_type=f32)
    grad_out = cotangent.reshape(-1, model_width)
    grad_res = grad_out.astype(f32)
    grad_down_t = jnp.einsum("rd,rf->df", grad_out, mixed_act, preferred_element_type=f32)
    grad_mixed = jnp.einsum("rd,fd->rf", grad_out, w_ffn_down, preferred_element_type=f32)
    grad_gate = (grad_mixed * ffn_up * silu_grad(ffn_gate)).astype(bf16)
    grad_up = (grad_mixed * jax.nn.silu(ffn_gate)).astype(bf16)
    grad_pair = jnp.concatenate([grad_gate, grad_up], axis=1)
    grad_pair_w = jnp.einsum("rd,rf->df", normed_two, grad_pair, preferred_element_type=f32)
    ffn_part = jnp.einsum(
        "rf,df->rd", grad_gate, w_ffn_gate, preferred_element_type=f32
    ) + jnp.einsum("rf,df->rd", grad_up, w_ffn_up, preferred_element_type=f32)
    (grad_normed_two, ffn_sum), (pair_rows, down_rows) = summed_arrays(
        [ffn_part, ffn_down_part], [grad_pair_w, grad_down_t], 0, 2, "sum_ffn"
    )
    result = (hidden_res + ffn_sum).astype(bf16).reshape(inputs.shape)
    grad_two_rows, grad_gain_two = norm_back(hidden_res, scale_two, norm_gain2, grad_normed_two)
    grad_hidden = grad_res + grad_two_rows
    grad_attn = grad_hidden.astype(bf16)
    grad_out_t = jnp.einsum("rd,rv->dv", grad_attn, gated_bf, preferred_element_type=f32)
    grad_gated = jnp.einsum("rd,vd->rv", grad_attn, w_output, preferred_element_type=f32).reshape(
        -1, heads_here, value_dim
    )
    grad_outputs, grad_gain_head_part, grad_gate_heads = gate_pull(grad_gated)
    grad_outputs = grad_outputs.reshape(-1, heads_here * value_dim)
    back_pair = stacked(
        [
            jnp.concatenate(
                [
                    jnp.einsum(
                        "tk,tv->kv", core[1], one(grad_outputs, s, h, value_dim), precision=HIGHEST
                    ),
                    core[3][:, value_dim:],
                ],
                axis=1,
            )
            for core, (s, h) in zip(cores, pairs)
        ]
    )
    later_all = exchange(back_pair, value_dim, True, 3)
    pulled = [
        gla_backward(
            one(queries, s, h, key_dim),
            one(keys_proj, s, h, key_dim),
            one(values_proj, s, h, value_dim),
            one(log_rates, s, h, key_dim),
            cores[i][2],
            entries[i],
            later_all[i * key_dim : (i + 1) * key_dim],
            one(grad_outputs, s, h, value_dim),
        )
        for i, (s, h) in enumerate(pairs)
    ]
    grad_q_all, grad_k_all, grad_v_all, grad_lr_all = (
        join([pull[j] for pull in pulled]) for j in range(4)
    )
    grad_logits = grad_lr_all * jax.nn.sigmoid(-logits) / GATE_NORM
    grad_bias = jnp.sum(grad_logits, axis=0)
    grad_low_up = jnp.einsum("rc,rk->ck", low_rank, grad_logits, precision=HIGHEST)
    grad_low = jnp.einsum("rk,ck->rc", grad_logits, w_low_up.astype(f32), precision=HIGHEST)
    grad_low_down_part = jnp.einsum(
        "rd,rc->dc", normed_one.astype(f32), grad_low, precision=HIGHEST
    )
    grad_q = (grad_q_all * key_scale).astype(bf16)
    grad_k = grad_k_all.astype(bf16)
    grad_v = grad_v_all.astype(bf16)
    grad_g = grad_gate_heads.reshape(-1, heads_here * value_dim).astype(bf16)
    grad_proj = jnp.concatenate([grad_q, grad_k, grad_v, grad_g], axis=1)
    grad_proj_w = jnp.einsum("rd,rk->dk", normed_one, grad_proj, preferred_element_type=f32)
    attn_part = (
        jnp.einsum("rk,dk->rd", grad_q, w_query, preferred_element_type=f32)
        + jnp.einsum("rk,dk->rd", grad_k, w_key, preferred_element_type=f32)
        + jnp.einsum("rv,dv->rd", grad_v, w_value, preferred_element_type=f32)
        + jnp.einsum("rv,dv->rd", grad_g, w_gate_out, preferred_element_type=f32)
        + jnp.einsum("rc,dc->rd", grad_low, w_low_down.astype(f32), precision=HIGHEST)
    )
    gain_one_part = jnp.sum(attn_part * rows_in * scale_one, axis=0)
    owners = lax.axis_size("context") * lax.axis_size("dp")

    def packed_rows(parts):
        flat = jnp.concatenate(parts, axis=1)
        padded = -(-flat.shape[1] // 1024) * 1024
        flat = jnp.pad(flat, ((0, 0), (0, padded - flat.shape[1])))
        return flat.reshape(owners, -1, 128)

    rank = low_rank.shape[1]
    width_up = w_low_up.shape[1]
    tensor_pack = packed_rows(
        [
            grad_low_down_part.reshape(owners, -1),
            gain_one_part.reshape(owners, -1),
            grad_gain_head_part.reshape(owners, -1),
        ]
    )
    local_pack = packed_rows(
        [
            grad_gain_two.reshape(owners, -1),
            grad_low_up.reshape(rank, owners, -1).transpose(1, 0, 2).reshape(owners, -1),
            grad_bias.reshape(owners, -1),
        ]
    )
    pack = jnp.concatenate([tensor_pack, local_pack], axis=1)
    tail = tensor_pack.shape[1]
    (grad_normed_one,), (proj_rows, out_rows, pack_rows) = summed_arrays(
        [attn_part], [grad_proj_w, grad_out_t, pack.reshape(-1, 128)], tail, 4, "sum_attn_back"
    )
    grad_one_rows, _ = norm_back(rows_in, scale_one, norm_gain1, grad_normed_one)
    grad_inputs = (grad_hidden + grad_one_rows).reshape(inputs.shape)
    flat_ten, flat_own = pack_rows[:tail].reshape(-1), pack_rows[tail:].reshape(-1)
    part_model = model_width // owners
    part_head = value_dim // owners
    part_up = width_up // owners
    grad_w_low_down = flat_ten[: part_model * rank].reshape(part_model, rank)
    grad_gain1 = flat_ten[part_model * rank : part_model * (rank + 1)]
    grad_head_gain = flat_ten[part_model * (rank + 1) : part_model * (rank + 1) + part_head]
    grad_gain2 = flat_own[:part_model]
    grad_w_low_up = flat_own[part_model : part_model + rank * part_up].reshape(rank, part_up)
    grad_forget_bias = flat_own[part_model + rank * part_up : part_model + (rank + 1) * part_up]
    width_q = heads_here * key_dim
    width_v = heads_here * value_dim
    grad_w_query = proj_rows[:, :width_q]
    grad_w_key = proj_rows[:, width_q : 2 * width_q]
    grad_w_value = proj_rows[:, 2 * width_q : 2 * width_q + width_v]
    grad_w_gate_out = proj_rows[:, 2 * width_q + width_v :]
    grad_w_output = out_rows.T
    width_ffn = w_ffn_gate.shape[1]
    grad_w_ffn_gate = pair_rows[:, :width_ffn]
    grad_w_ffn_up = pair_rows[:, width_ffn:]
    grad_w_ffn_down = down_rows.T
    return (
        result,
        grad_inputs,
        grad_gain1,
        grad_w_query,
        grad_w_key,
        grad_w_value,
        grad_w_gate_out,
        grad_w_low_down,
        grad_w_low_up,
        grad_forget_bias,
        grad_head_gain,
        grad_w_output,
        grad_gain2,
        grad_w_ffn_gate,
        grad_w_ffn_up,
        grad_w_ffn_down,
    )


def solution(mesh):
    return jax.shard_map(
        shards,
        mesh=mesh,
        in_specs=(
            P("dp", "context", None),
            P(),
            P(None, "tensor"),
            P(None, "tensor"),
            P(None, "tensor"),
            P(None, "tensor"),
            P(),
            P(None, "tensor"),
            P("tensor"),
            P(),
            P("tensor", None),
            P(),
            P(None, "tensor"),
            P(None, "tensor"),
            P("tensor", None),
            P("dp", "context", None),
        ),
        out_specs=(
            P("dp", "context", None),
            P("dp", "context", None),
            P(("context", "dp")),
            P(("context", "dp"), "tensor"),
            P(("context", "dp"), "tensor"),
            P(("context", "dp"), "tensor"),
            P(("context", "dp"), "tensor"),
            P(("context", "dp"), None),
            P(None, ("tensor", "context", "dp")),
            P(("tensor", "context", "dp")),
            P(("context", "dp")),
            P("tensor", ("context", "dp")),
            P(("context", "dp")),
            P(("context", "dp"), "tensor"),
            P(("context", "dp"), "tensor"),
            P("tensor", ("context", "dp")),
        ),
        check_vma=False,
    )
```

```python
import functools

import jax
import jax.numpy as jnp
from jax import lax
from jax.experimental import pallas as pl
from jax.experimental.pallas import tpu as pltpu
from jax.sharding import PartitionSpec as P

BLOCK = 64


EPS_MODEL = 1e-06
EPS_HEAD = 1e-05
GATE_NORM = 16.0
HIGHEST = lax.Precision.HIGHEST


VMEM_LIMIT = 60 * 1024 * 1024
VMEM = pltpu.MemorySpace.VMEM
MESH_ID = pl.DeviceIdType.MESH


def hdot(left, right, dims):
    return lax.dot_general(
        left, right, (dims, ((), ())), precision=HIGHEST, preferred_element_type=jnp.float32
    )


def column_of(row, height):
    return jnp.broadcast_to(row, (height, row.shape[1])).T


def triangle(length):
    rows = lax.broadcasted_iota(jnp.int32, (length, length), 0)
    cols = lax.broadcasted_iota(jnp.int32, (length, length), 1)
    return rows >= cols


def gla_forward_kernel(q_ref, k_ref, v_ref, r_ref, out_ref, decayed_ref, states_ref, pair_ref):
    tokens, key_dim = q_ref.shape
    value_dim = v_ref.shape[1]
    causal = triangle(BLOCK)
    ones_low = causal.astype(jnp.float32)
    state = jnp.zeros((key_dim, value_dim), jnp.float32)
    before = jnp.zeros((1, key_dim), jnp.float32)
    for block in range(tokens // BLOCK):
        span = pl.ds(block * BLOCK, BLOCK)
        queries, keys_in, values_in = q_ref[span, :], k_ref[span, :], v_ref[span, :]
        cumul = hdot(ones_low, r_ref[span, :], ((1,), (0,)))
        end_log = cumul[BLOCK - 1 :, :]
        anchor = 0.5 * end_log
        scores = hdot(
            queries * jnp.exp(cumul - anchor), keys_in * jnp.exp(anchor - cumul), ((1,), (1,))
        )
        scores = jnp.where(causal, scores, 0.0)
        out_ref[span, :] = hdot(scores, values_in, ((1,), (0,))) + hdot(
            queries * jnp.exp(cumul), state, ((1,), (0,))
        )
        decayed_ref[span, :] = queries * jnp.exp(cumul + before)
        states_ref[block] = state
        added = hdot(keys_in * jnp.exp(end_log - cumul), values_in, ((0,), (0,)))
        state = column_of(jnp.exp(end_log), key_dim)[:, :1] * state + added
        before = before + end_log
    pair_ref[:, :value_dim] = state
    pair_ref[:, value_dim:] = column_of(jnp.exp(before), key_dim)


def gla_forward(queries, keys_in, values_in, log_rates):
    tokens, key_dim = queries.shape
    value_dim = values_in.shape[1]
    f32 = jnp.float32
    return pl.pallas_call(
        gla_forward_kernel,
        out_shape=(
            jax.ShapeDtypeStruct((tokens, value_dim), f32),
            jax.ShapeDtypeStruct((tokens, key_dim), f32),
            jax.ShapeDtypeStruct((tokens // BLOCK, key_dim, value_dim), f32),
            jax.ShapeDtypeStruct((key_dim, value_dim + key_dim), f32),
        ),
        compiler_params=pltpu.CompilerParams(vmem_limit_bytes=VMEM_LIMIT),
        name="gla_forward",
    )(queries, keys_in, values_in, log_rates)


def gla_backward_kernel(
    q_ref, k_ref, v_ref, r_ref, states_ref, entry_ref, later_ref, g_ref, dq_ref, dk_ref, dv_ref, dr_ref
):
    tokens, key_dim = q_ref.shape
    causal = triangle(BLOCK)
    ones_low = causal.astype(jnp.float32)
    blocks = tokens // BLOCK
    cumuls, befores = [], []
    before = jnp.zeros((1, key_dim), jnp.float32)
    for block in range(blocks):
        cumul = hdot(ones_low, r_ref[pl.ds(block * BLOCK, BLOCK), :], ((1,), (0,)))
        cumuls.append(cumul)
        befores.append(before)
        before = before + cumul[BLOCK - 1 :, :]
    grad_state = later_ref[...]
    entry = entry_ref[...]
    for block in reversed(range(blocks)):
        span = pl.ds(block * BLOCK, BLOCK)
        queries, keys_in, values_in = q_ref[span, :], k_ref[span, :], v_ref[span, :]
        grad_out = g_ref[span, :]
        cumul = cumuls[block]
        end_log = cumul[BLOCK - 1 :, :]
        anchor = 0.5 * end_log
        state = states_ref[block] + column_of(jnp.exp(befores[block]), key_dim)[:, :1] * entry
        up, down = jnp.exp(cumul - anchor), jnp.exp(anchor - cumul)
        grow, rest = jnp.exp(cumul), jnp.exp(end_log - cumul)
        q_up, k_down = queries * up, keys_in * down
        scores = jnp.where(causal, hdot(q_up, k_down, ((1,), (1,))), 0.0)
        grad_scores = jnp.where(causal, hdot(grad_out, values_in, ((1,), (1,))), 0.0)
        grad_q = hdot(grad_scores, k_down, ((1,), (0,))) * up + grow * hdot(
            grad_out, state, ((1,), (1,))
        )
        carried_k = hdot(values_in, grad_state, ((1,), (1,))) * rest
        grad_k = hdot(grad_scores, q_up, ((0,), (0,))) * down + carried_k
        dv_ref[span, :] = hdot(scores, grad_out, ((0,), (0,))) + hdot(
            keys_in * rest, grad_state, ((1,), (0,))
        )
        dq_ref[span, :] = grad_q
        dk_ref[span, :] = grad_k
        grad_cumul = queries * grad_q - keys_in * grad_k
        end_column = column_of(jnp.exp(end_log), key_dim)
        state_term = jnp.sum(grad_state * state, axis=1, keepdims=True) * end_column
        grad_end = state_term.T[:1, :] + jnp.sum(carried_k * keys_in, axis=0, keepdims=True)
        dr_ref[span, :] = hdot(ones_low, grad_cumul, ((0,), (0,))) + grad_end
        grad_state = end_column[:, :1] * grad_state + hdot(
            queries * grow, grad_out, ((0,), (0,))
        )


def gla_backward(queries, keys_in, values_in, log_rates, states, entry, later, grad_out):
    shaped = tuple(
        jax.ShapeDtypeStruct(part.shape, jnp.float32)
        for part in (queries, keys_in, values_in, log_rates)
    )
    return pl.pallas_call(
        gla_backward_kernel,
        out_shape=shaped,
        compiler_params=pltpu.CompilerParams(vmem_limit_bytes=VMEM_LIMIT),
        name="gla_backward",
    )(queries, keys_in, values_in, log_rates, states, entry, later, grad_out)


def exchange_kernel(size, reverse, value_dim, pair_ref, out_ref, slots, send_sem, recv_sem):
    here = lax.axis_index("context")
    barrier = pltpu.get_barrier_semaphore()
    for step in range(1, size):
        peer = lax.rem(here + step, size)
        pl.semaphore_signal(barrier, inc=1, device_id={"context": peer}, device_id_type=MESH_ID)
    pl.semaphore_wait(barrier, size - 1)
    copies = []
    for step in range(1, size):
        peer = lax.rem(here + step, size)
        copies.append(
            pltpu.make_async_remote_copy(
                src_ref=pair_ref,
                dst_ref=slots.at[step - 1],
                send_sem=send_sem.at[step - 1],
                recv_sem=recv_sem.at[step - 1],
                device_id={"context": peer},
                device_id_type=MESH_ID,
            )
        )
    for copy in copies:
        copy.start()
    for copy in copies:
        copy.wait()
    out_ref[...] = jnp.zeros_like(out_ref)
    order = range(1, size) if reverse else reversed(range(1, size))
    if reverse:
        for m in reversed(range(1, size)):

            @pl.when(here + m < size)
            def _(m=m):
                part = slots.at[size - m - 1]
                out_ref[...] = part[:, value_dim : value_dim + 1] * out_ref[...] + part[:, :value_dim]
    else:
        for step in order:

            @pl.when(here >= step)
            def _(step=step):
                part = slots.at[step - 1]
                out_ref[...] = part[:, value_dim : value_dim + 1] * out_ref[...] + part[:, :value_dim]


def exchange(pair, value_dim, reverse, collective_id):
    size = lax.axis_size("context")
    return pl.pallas_call(
        functools.partial(exchange_kernel, size, reverse, value_dim),
        out_shape=jax.ShapeDtypeStruct((pair.shape[0], value_dim), jnp.float32),
        in_specs=[pl.BlockSpec(memory_space=VMEM)],
        out_specs=pl.BlockSpec(memory_space=VMEM),
        scratch_shapes=[
            pltpu.VMEM((size - 1,) + pair.shape, jnp.float32),
            pltpu.SemaphoreType.DMA((size - 1,)),
            pltpu.SemaphoreType.DMA((size - 1,)),
        ],
        compiler_params=pltpu.CompilerParams(
            collective_id=collective_id, has_side_effects=True, vmem_limit_bytes=VMEM_LIMIT
        ),
        name="exchange_back" if reverse else "exchange",
    )(pair)


def sums_kernel(sizes, n_all, pieces, made, tail, *refs):
    n_ctx, n_dp, n_ten = sizes
    n_sc = len(pieces)
    take = iter(refs)
    all_in = [next(take) for _ in range(n_all)]
    factors = [(next(take), next(take) if is_made else None) for is_made in made]
    all_out = [next(take) for _ in range(n_all)]
    sc_out = [next(take) for _ in range(n_sc)]
    all_slots = [next(take) for _ in range(n_all)]
    all_sems = [next(take) for _ in range(n_all)]
    near = [next(take) for _ in range(n_sc)]
    near_sems = [next(take) for _ in range(n_sc)]
    line = [next(take) for _ in range(n_sc)]
    line_sems = [next(take) for _ in range(n_sc)]
    sc_in = [next(take) if right is not None else left for left, right in factors]
    if tail:
        tail_slots, tail_sems = next(take), next(take)
    ctx = lax.axis_index("context")
    dp = lax.axis_index("dp")
    ten = lax.axis_index("tensor")
    use_ten = n_all > 0 or tail

    def peers(index, size):
        return [lax.rem(index + step, size) for step in range(1, size)]

    def remote(src, dst, sems, at, axis, peer):
        return pltpu.make_async_remote_copy(
            src_ref=src,
            dst_ref=dst,
            send_sem=sems.at[(0,) + at],
            recv_sem=sems.at[(1,) + at],
            device_id={axis: peer},
            device_id_type=MESH_ID,
        )

    barrier = pltpu.get_barrier_semaphore()

    def greet(axis, peer):
        pl.semaphore_signal(barrier, inc=1, device_id={axis: peer}, device_id_type=MESH_ID)

    expect = 0
    if n_sc:
        for peer in peers(ctx, n_ctx):
            greet("context", peer)
        expect += n_ctx - 1
    if use_ten:
        for peer in peers(ten, n_ten):
            greet("tensor", peer)
        expect += n_ten - 1
    if n_sc:

        @pl.when(dp > 0)
        def _():
            greet("dp", dp - 1)

        @pl.when(dp < n_dp - 1)
        def _():
            greet("dp", dp + 1)

    if n_sc:
        inner = jnp.logical_and(dp > 0, dp < n_dp - 1)

        @pl.when(inner)
        def _():
            pl.semaphore_wait(barrier, expect + 2)

        @pl.when(jnp.logical_not(inner))
        def _():
            pl.semaphore_wait(barrier, expect + 1)

    else:
        pl.semaphore_wait(barrier, expect)

    def rows(i, piece):
        height = sc_in[i].shape[1] // pieces[i]
        return pl.ds(piece * height, height)

    def near_copy(i, step, dest, piece):
        peer = lax.rem(ctx + step, n_ctx)
        return remote(
            sc_in[i].at[peer * n_dp + dest, rows(i, piece)],
            near[i].at[step - 1, dest, rows(i, piece)],
            near_sems[i],
            (step - 1, dest, piece),
            "context",
            peer,
        )

    def line_copy(i, way, dest, piece, peer):
        place = line[i].at[way, dest, rows(i, piece)]
        return remote(place, place, line_sems[i], (way, dest, piece), "dp", peer)

    def all_copy(i, step):
        peer = lax.rem(ten + step, n_ten)
        return remote(
            all_in[i].at[peer], all_slots[i].at[step - 1], all_sems[i], (0, step - 1), "tensor", peer
        )

    def all_share(i, step):
        peer = lax.rem(ten + step, n_ten)
        return remote(
            all_out[i].at[ten], all_out[i].at[ten], all_sems[i], (1, step - 1), "tensor", peer
        )

    def over_pieces(i, body):
        if pieces[i] == 1:
            body(0)
        else:

            def lap(piece, carry):
                body(piece)
                return carry

            lax.fori_loop(0, pieces[i], lap, 0)

    order = []
    for k in range(n_dp):
        for dest in (n_dp - 1 - k, k):
            if dest not in order:
                order.append(dest)
    for i in range(n_all):
        for step in range(1, n_ten):
            all_copy(i, step).start()
    def make(i, owner):
        left, right = factors[i]
        if right is not None:
            sc_in[i][owner] = jnp.dot(
                left[owner], right[...], preferred_element_type=jnp.float32
            )

    for dest in order:
        for i in range(n_sc):
            for step in range(1, n_ctx):
                make(i, lax.rem(ctx + step, n_ctx) * n_dp + dest)
                over_pieces(i, lambda piece: near_copy(i, step, dest, piece).start())
            make(i, ctx * n_dp + dest)

    def own_sum(i, dest, piece):
        total = sc_in[i][ctx * n_dp + dest, rows(i, piece)]
        for step in range(1, n_ctx):
            near_copy(i, step, dest, piece).wait_recv()
            total = total + near[i][step - 1, dest, rows(i, piece)]
        return total

    def pass_on(i, way, dest, piece):
        forward = way == 0
        active = dp < dest if forward else dp > dest
        first = dp == (0 if forward else n_dp - 1)
        peer = dp + 1 if forward else dp - 1
        back = dp - 1 if forward else dp + 1

        @pl.when(active)
        def _():
            own = own_sum(i, dest, piece)

            @pl.when(first)
            def _():
                line[i][way, dest, rows(i, piece)] = own

            @pl.when(jnp.logical_not(first))
            def _():
                line_copy(i, way, dest, piece, back).wait_recv()
                line[i][way, dest, rows(i, piece)] = line[i][way, dest, rows(i, piece)] + own

            line_copy(i, way, dest, piece, peer).start()

    def reduce_all():
        for i in range(n_all):
            total = all_in[i][ten]
            for step in range(1, n_ten):
                all_copy(i, step).wait_recv()
                total = total + all_slots[i][step - 1]
            all_out[i][ten] = total
            for step in range(1, n_ten):
                all_share(i, step).start()

    if not n_sc:
        reduce_all()
    else:
        for k in range(n_dp - 1):

            def both(piece, i, k=k):
                pass_on(i, 0, n_dp - 1 - k, piece)
                pass_on(i, 1, k, piece)

            for i in range(n_sc):
                over_pieces(i, functools.partial(both, i=i))
            if k == 0:
                reduce_all()

    for i in range(n_sc):

        def finish(piece, i=i):
            sc_out[i][rows(i, piece), :] = own_sum(i, dp, piece)

            @pl.when(dp > 0)
            def _():
                line_copy(i, 0, dp, piece, dp - 1).wait_recv()
                sc_out[i][rows(i, piece), :] += line[i][0, dp, rows(i, piece)]

            @pl.when(dp < n_dp - 1)
            def _():
                line_copy(i, 1, dp, piece, dp + 1).wait_recv()
                sc_out[i][rows(i, piece), :] += line[i][1, dp, rows(i, piece)]

        over_pieces(i, finish)

    if tail:
        last = sc_out[n_sc - 1]
        tail_slots[ten] = last[:tail, :]

        def tail_copy(step):
            peer = lax.rem(ten + step, n_ten)
            return remote(
                tail_slots.at[ten], tail_slots.at[ten], tail_sems, (step - 1,), "tensor", peer
            )

        def tail_come(step):
            sender = lax.rem(ten + n_ten - step, n_ten)
            return remote(
                tail_slots.at[sender], tail_slots.at[sender], tail_sems, (step - 1,), "tensor", sender
            )

        for step in range(1, n_ten):
            tail_copy(step).start()
        for step in range(1, n_ten):
            tail_come(step).wait_recv()
        total = tail_slots[0]
        for index in range(1, n_ten):
            total = total + tail_slots[index]
        last[:tail, :] = total
        for step in range(1, n_ten):
            tail_copy(step).wait_send()

    for i in range(n_all):
        for step in range(1, n_ten):
            all_copy(i, step).wait_send()
            sender = lax.rem(ten + n_ten - step, n_ten)
            remote(
                all_out[i].at[sender],
                all_out[i].at[sender],
                all_sems[i],
                (1, step - 1),
                "tensor",
                sender,
            ).wait_recv()
            all_share(i, step).wait_send()
    for i in range(n_sc):
        for dest in range(n_dp):

            def drain(piece, i=i, dest=dest):
                for step in range(1, n_ctx):
                    near_copy(i, step, dest, piece).wait_send()

                @pl.when(dp < dest)
                def _():
                    line_copy(i, 0, dest, piece, dp + 1).wait_send()

                @pl.when(dp > dest)
                def _():
                    line_copy(i, 1, dest, piece, dp - 1).wait_send()

            over_pieces(i, drain)


def summed_arrays(whole, scattered, tail, collective_id, name):
    n_ctx, n_dp, n_ten = (lax.axis_size(axis) for axis in ("context", "dp", "tensor"))
    owners = n_ctx * n_dp
    f32 = jnp.float32
    whole_in = [part.reshape(n_ten, part.shape[0] // n_ten, part.shape[1]) for part in whole]
    made = tuple(isinstance(part, tuple) for part in scattered)
    operands, sc_in = [], []
    for part in scattered:
        left, right = part if isinstance(part, tuple) else (part, None)
        blocks = left.reshape(owners, left.shape[0] // owners, left.shape[1])
        operands += [blocks] if right is None else [blocks, right]
        width = left.shape[1] if right is None else right.shape[1]
        sc_in.append(jax.ShapeDtypeStruct(blocks.shape[:2] + (width,), f32))
    pieces = []
    for part in sc_in:
        count = 4
        while part.shape[1] % (count * 8):
            count //= 2
        pieces.append(count if part.shape[2] > 128 else 1)
    scratch = [pltpu.VMEM((n_ten - 1,) + part.shape[1:], f32) for part in whole_in]
    scratch += [pltpu.SemaphoreType.DMA((2, 2, n_ten - 1)) for _ in whole_in]
    scratch += [pltpu.VMEM((n_ctx - 1, n_dp) + part.shape[1:], f32) for part in sc_in]
    scratch += [pltpu.SemaphoreType.DMA((2, n_ctx - 1, n_dp, count)) for count in pieces]
    scratch += [pltpu.VMEM((2, n_dp) + part.shape[1:], f32) for part in sc_in]
    scratch += [pltpu.SemaphoreType.DMA((2, 2, n_dp, count)) for count in pieces]
    scratch += [pltpu.VMEM(part.shape, f32) for part, is_made in zip(sc_in, made) if is_made]
    if tail:
        scratch += [
            pltpu.VMEM((n_ten, tail, scattered[-1].shape[1]), f32),
            pltpu.SemaphoreType.DMA((2, n_ten - 1)),
        ]
    outs = pl.pallas_call(
        functools.partial(sums_kernel, (n_ctx, n_dp, n_ten), len(whole), tuple(pieces), made, tail),
        out_shape=tuple(
            [jax.ShapeDtypeStruct(part.shape, f32) for part in whole_in]
            + [jax.ShapeDtypeStruct(part.shape[1:], f32) for part in sc_in]
        ),
        in_specs=[pl.BlockSpec(memory_space=VMEM)] * (len(whole) + len(operands)),
        out_specs=tuple([pl.BlockSpec(memory_space=VMEM)] * (len(whole) + len(scattered))),
        scratch_shapes=scratch,
        compiler_params=pltpu.CompilerParams(
            collective_id=collective_id, has_side_effects=True, vmem_limit_bytes=VMEM_LIMIT
        ),
        name=name,
    )(*whole_in, *operands)
    totals = [out.reshape(part.shape) for out, part in zip(outs, whole)]
    return totals, list(outs[len(whole) :])


def rms_scale(rows_in):
    return lax.rsqrt(jnp.mean(rows_in * rows_in, axis=-1, keepdims=True) + EPS_MODEL)


def norm_back(rows_in, scale_rows, gain_in, grad_normed):
    weighted = gain_in * grad_normed
    grad_gain = jnp.sum(grad_normed * rows_in * scale_rows, axis=0)
    grad_rows = scale_rows * (
        weighted
        - rows_in * scale_rows * scale_rows * jnp.mean(weighted * rows_in, axis=-1, keepdims=True)
    )
    return (grad_rows, grad_gain)


def head_gate(outputs, head_gain, gate_in):
    scale_rows = lax.rsqrt(jnp.mean(outputs * outputs, axis=-1, keepdims=True) + EPS_HEAD)
    return outputs * scale_rows * head_gain * jax.nn.silu(gate_in)


def silu_grad(values_in):
    sigmoid_v = jax.nn.sigmoid(values_in)
    return sigmoid_v * (1.0 + values_in * (1.0 - sigmoid_v))


def shards(
    inputs,
    norm_gain1,
    w_query,
    w_key,
    w_value,
    w_gate_out,
    w_low_down,
    w_low_up,
    forget_bias,
    head_gain,
    w_output,
    norm_gain2,
    w_ffn_gate,
    w_ffn_up,
    w_ffn_down,
    cotangent,
):
    bf16 = jnp.bfloat16
    f32 = jnp.float32
    seqs_here, tok_here, model_width = inputs.shape
    value_dim = head_gain.shape[0]
    heads_here = w_output.shape[0] // value_dim
    key_dim = w_query.shape[1] // heads_here
    key_scale = key_dim ** (-0.5)
    rows_in = inputs.reshape(-1, model_width).astype(f32)
    scale_one = rms_scale(rows_in)
    normed_one = (rows_in * scale_one * norm_gain1).astype(bf16)
    queries = jnp.dot(normed_one, w_query, preferred_element_type=f32) * key_scale
    keys_proj = jnp.dot(normed_one, w_key, preferred_element_type=f32)
    values_proj = jnp.dot(normed_one, w_value, preferred_element_type=f32)
    gate_in = jnp.dot(normed_one, w_gate_out, preferred_element_type=f32)
    low_rank = jnp.dot(normed_one, w_low_down, preferred_element_type=f32)
    logits = jnp.dot(low_rank, w_low_up.astype(f32), precision=HIGHEST) + forget_bias
    log_rates = jax.nn.log_sigmoid(logits) / GATE_NORM
    pairs = [(s, h) for s in range(seqs_here) for h in range(heads_here)]

    def one(packed, s, h, width):
        return packed[s * tok_here : (s + 1) * tok_here, h * width : (h + 1) * width]

    def join(parts):
        return jnp.concatenate(
            [
                jnp.concatenate(parts[s * heads_here : (s + 1) * heads_here], axis=1)
                for s in range(seqs_here)
            ],
            axis=0,
        )

    def stacked(parts):
        return jnp.concatenate(parts, axis=0)

    cores = [
        gla_forward(
            one(queries, s, h, key_dim),
            one(keys_proj, s, h, key_dim),
            one(values_proj, s, h, value_dim),
            one(log_rates, s, h, key_dim),
        )
        for s, h in pairs
    ]
    pair_all = stacked([core[3] for core in cores])
    entry_all = exchange(pair_all, value_dim, False, 0)
    entries = [entry_all[i * key_dim : (i + 1) * key_dim] for i in range(len(pairs))]
    outputs = join(
        [
            core[0] + jnp.dot(core[1], entry, precision=HIGHEST)
            for core, entry in zip(cores, entries)
        ]
    ).reshape(-1, heads_here, value_dim)
    gate_heads = gate_in.reshape(-1, heads_here, value_dim)
    gated, gate_pull = jax.vjp(head_gate, outputs, head_gain, gate_heads)
    gated_bf = gated.reshape(-1, heads_here * value_dim).astype(bf16)
    attn_part_out = jnp.dot(gated_bf, w_output, preferred_element_type=f32)
    (attn_sum,), _ = summed_arrays([attn_part_out], [], 0, 1, "sum_attn")
    hidden_res = rows_in + attn_sum
    scale_two = rms_scale(hidden_res)
    normed_two = (hidden_res * scale_two * norm_gain2).astype(bf16)
    ffn_gate = jnp.dot(normed_two, w_ffn_gate, preferred_element_type=f32)
    ffn_up = jnp.dot(normed_two, w_ffn_up, preferred_element_type=f32)
    mixed_act = (jax.nn.silu(ffn_gate) * ffn_up).astype(bf16)
    ffn_down_part = jnp.dot(mixed_act, w_ffn_down, preferred_element_type=f32)
    grad_out = cotangent.reshape(-1, model_width)
    grad_res = grad_out.astype(f32)
    grad_mixed = jnp.einsum("rd,fd->rf", grad_out, w_ffn_down, preferred_element_type=f32)
    grad_gate = (grad_mixed * ffn_up * silu_grad(ffn_gate)).astype(bf16)
    grad_up = (grad_mixed * jax.nn.silu(ffn_gate)).astype(bf16)
    grad_pair = jnp.concatenate([grad_gate, grad_up], axis=1)
    ffn_part = jnp.einsum(
        "rf,df->rd", grad_gate, w_ffn_gate, preferred_element_type=f32
    ) + jnp.einsum("rf,df->rd", grad_up, w_ffn_up, preferred_element_type=f32)
    (grad_normed_two, ffn_sum), (pair_rows, down_rows) = summed_arrays(
        [ffn_part, ffn_down_part], [(normed_two.T, grad_pair), (grad_out.T, mixed_act)], 0, 2, "sum_ffn"
    )
    result = (hidden_res + ffn_sum).astype(bf16).reshape(inputs.shape)
    grad_two_rows, grad_gain_two = norm_back(hidden_res, scale_two, norm_gain2, grad_normed_two)
    grad_hidden = grad_res + grad_two_rows
    grad_attn = grad_hidden.astype(bf16)
    grad_gated = jnp.einsum("rd,vd->rv", grad_attn, w_output, preferred_element_type=f32).reshape(
        -1, heads_here, value_dim
    )
    grad_outputs, grad_gain_head_part, grad_gate_heads = gate_pull(grad_gated)
    grad_outputs = grad_outputs.reshape(-1, heads_here * value_dim)
    back_pair = stacked(
        [
            jnp.concatenate(
                [
                    jnp.einsum(
                        "tk,tv->kv", core[1], one(grad_outputs, s, h, value_dim), precision=HIGHEST
                    ),
                    core[3][:, value_dim:],
                ],
                axis=1,
            )
            for core, (s, h) in zip(cores, pairs)
        ]
    )
    later_all = exchange(back_pair, value_dim, True, 3)
    pulled = [
        gla_backward(
            one(queries, s, h, key_dim),
            one(keys_proj, s, h, key_dim),
            one(values_proj, s, h, value_dim),
            one(log_rates, s, h, key_dim),
            cores[i][2],
            entries[i],
            later_all[i * key_dim : (i + 1) * key_dim],
            one(grad_outputs, s, h, value_dim),
        )
        for i, (s, h) in enumerate(pairs)
    ]
    grad_q_all, grad_k_all, grad_v_all, grad_lr_all = (
        join([pull[j] for pull in pulled]) for j in range(4)
    )
    grad_logits = grad_lr_all * jax.nn.sigmoid(-logits) / GATE_NORM
    grad_bias = jnp.sum(grad_logits, axis=0)
    grad_low_up = jnp.einsum("rc,rk->ck", low_rank, grad_logits, precision=HIGHEST)
    grad_low = jnp.einsum("rk,ck->rc", grad_logits, w_low_up.astype(f32), precision=HIGHEST)
    grad_low_down_part = jnp.einsum(
        "rd,rc->dc", normed_one.astype(f32), grad_low, precision=HIGHEST
    )
    grad_q = (grad_q_all * key_scale).astype(bf16)
    grad_k = grad_k_all.astype(bf16)
    grad_v = grad_v_all.astype(bf16)
    grad_g = grad_gate_heads.reshape(-1, heads_here * value_dim).astype(bf16)
    grad_proj = jnp.concatenate([grad_q, grad_k, grad_v, grad_g], axis=1)
    attn_part = (
        jnp.einsum("rk,dk->rd", grad_q, w_query, preferred_element_type=f32)
        + jnp.einsum("rk,dk->rd", grad_k, w_key, preferred_element_type=f32)
        + jnp.einsum("rv,dv->rd", grad_v, w_value, preferred_element_type=f32)
        + jnp.einsum("rv,dv->rd", grad_g, w_gate_out, preferred_element_type=f32)
        + jnp.einsum("rc,dc->rd", grad_low, w_low_down.astype(f32), precision=HIGHEST)
    )
    gain_one_part = jnp.sum(attn_part * rows_in * scale_one, axis=0)
    owners = lax.axis_size("context") * lax.axis_size("dp")

    def packed_rows(parts):
        flat = jnp.concatenate(parts, axis=1)
        padded = -(-flat.shape[1] // 1024) * 1024
        flat = jnp.pad(flat, ((0, 0), (0, padded - flat.shape[1])))
        return flat.reshape(owners, -1, 128)

    rank = low_rank.shape[1]
    width_up = w_low_up.shape[1]
    tensor_pack = packed_rows(
        [
            grad_low_down_part.reshape(owners, -1),
            gain_one_part.reshape(owners, -1),
            grad_gain_head_part.reshape(owners, -1),
        ]
    )
    local_pack = packed_rows(
        [
            grad_gain_two.reshape(owners, -1),
            grad_low_up.reshape(rank, owners, -1).transpose(1, 0, 2).reshape(owners, -1),
            grad_bias.reshape(owners, -1),
        ]
    )
    pack = jnp.concatenate([tensor_pack, local_pack], axis=1)
    tail = tensor_pack.shape[1]
    (grad_normed_one,), (proj_rows, out_rows, pack_rows) = summed_arrays(
        [attn_part],
        [(normed_one.T, grad_proj), (grad_attn.T, gated_bf), pack.reshape(-1, 128)],
        tail,
        4,
        "sum_attn_back",
    )
    grad_one_rows, _ = norm_back(rows_in, scale_one, norm_gain1, grad_normed_one)
    grad_inputs = (grad_hidden + grad_one_rows).reshape(inputs.shape)
    flat_ten, flat_own = pack_rows[:tail].reshape(-1), pack_rows[tail:].reshape(-1)
    part_model = model_width // owners
    part_head = value_dim // owners
    part_up = width_up // owners
    grad_w_low_down = flat_ten[: part_model * rank].reshape(part_model, rank)
    grad_gain1 = flat_ten[part_model * rank : part_model * (rank + 1)]
    grad_head_gain = flat_ten[part_model * (rank + 1) : part_model * (rank + 1) + part_head]
    grad_gain2 = flat_own[:part_model]
    grad_w_low_up = flat_own[part_model : part_model + rank * part_up].reshape(rank, part_up)
    grad_forget_bias = flat_own[part_model + rank * part_up : part_model + (rank + 1) * part_up]
    width_q = heads_here * key_dim
    width_v = heads_here * value_dim
    grad_w_query = proj_rows[:, :width_q]
    grad_w_key = proj_rows[:, width_q : 2 * width_q]
    grad_w_value = proj_rows[:, 2 * width_q : 2 * width_q + width_v]
    grad_w_gate_out = proj_rows[:, 2 * width_q + width_v :]
    grad_w_output = out_rows.T
    width_ffn = w_ffn_gate.shape[1]
    grad_w_ffn_gate = pair_rows[:, :width_ffn]
    grad_w_ffn_up = pair_rows[:, width_ffn:]
    grad_w_ffn_down = down_rows.T
    return (
        result,
        grad_inputs,
        grad_gain1,
        grad_w_query,
        grad_w_key,
        grad_w_value,
        grad_w_gate_out,
        grad_w_low_down,
        grad_w_low_up,
        grad_forget_bias,
        grad_head_gain,
        grad_w_output,
        grad_gain2,
        grad_w_ffn_gate,
        grad_w_ffn_up,
        grad_w_ffn_down,
    )


def solution(mesh):
    return jax.shard_map(
        shards,
        mesh=mesh,
        in_specs=(
            P("dp", "context", None),
            P(),
            P(None, "tensor"),
            P(None, "tensor"),
            P(None, "tensor"),
            P(None, "tensor"),
            P(),
            P(None, "tensor"),
            P("tensor"),
            P(),
            P("tensor", None),
            P(),
            P(None, "tensor"),
            P(None, "tensor"),
            P("tensor", None),
            P("dp", "context", None),
        ),
        out_specs=(
            P("dp", "context", None),
            P("dp", "context", None),
            P(("context", "dp")),
            P(("context", "dp"), "tensor"),
            P(("context", "dp"), "tensor"),
            P(("context", "dp"), "tensor"),
            P(("context", "dp"), "tensor"),
            P(("context", "dp"), None),
            P(None, ("tensor", "context", "dp")),
            P(("tensor", "context", "dp")),
            P(("context", "dp")),
            P("tensor", ("context", "dp")),
            P(("context", "dp")),
            P(("context", "dp"), "tensor"),
            P(("context", "dp"), "tensor"),
            P("tensor", ("context", "dp")),
        ),
        check_vma=False,
    )
```
